32 devices in a mesh: fsdp: 16 (over z, y, core), tp: 2 (over x).
Axes of the slice: x: 2, y: 2, z: 4, core: 2. Of those that a mesh axis runs over, the one named last changes fastest.
Arguments:
- grad_query: bfloat16 [2, 16, 2560, 768], P(None, 'fsdp', None, 'tp'), as said below
- grad_latent: bfloat16 [2, 16, 2560, 288], P(None, 'fsdp', None, 'tp'), as said below
- grad_gains: bfloat16 [2, 16, 1024], P(None, 'fsdp'), as said below
- param_query: float32 [2560, 768], P('fsdp', 'tp'), may hold values from -0.125 to 0.125
- param_latent: float32 [2560, 288], P('fsdp', 'tp'), may hold values from -0.125 to 0.125
- param_gains: float32 [1024], P('fsdp'), may hold values from -0.125 to 0.125
- first_query: float32 [2560, 768], P('fsdp', 'tp'), may hold values from -4 to 4
- first_latent: float32 [2560, 288], P('fsdp', 'tp'), may hold values from -4 to 4
- first_gains: float32 [1024], P('fsdp'), may hold values from -4 to 4
- second_query: float32 [2560, 768], P('fsdp', 'tp'), may hold values from 0.05 to 2
- second_latent: float32 [2560, 288], P('fsdp', 'tp'), may hold values from 0.05 to 2
- second_gains: float32 [1024], P('fsdp'), may hold values from 0.05 to 2
Outputs:
- new_query: float32 [2560, 768], P('fsdp', 'tp')
- new_latent: float32 [2560, 288], P('fsdp', 'tp')
- new_gains: float32 [1024], P('fsdp')
- next_first_query: float32 [2560, 768], P('fsdp', 'tp')
- next_first_latent: float32 [2560, 288], P('fsdp', 'tp')
- next_first_gains: float32 [1024], P('fsdp')
- next_second_query: float32 [2560, 768], P('fsdp', 'tp')
- next_second_latent: float32 [2560, 288], P('fsdp', 'tp')
- next_second_gains: float32 [1024], P('fsdp')
- train_query: bfloat16 [2560, 768], P(None, 'tp')
- train_latent: bfloat16 [2560, 288], P(None, 'tp')
- train_gains: bfloat16 [1024], replicated
The draws below stay inside these ranges and needn't reach their ends.
Inputs may be any that keep to these rules, and one draw needn't show every extreme that they name: `grad_query`: each device's gradient of its own tokens. `grad_latent`: each device's gradient of its own tokens. `grad_gains`: each device's gradient of its own tokens.
All inputs are finite; a program needn't handle non-finite values.
Results may differ from the reference program's by a relative error of at most 0.0004.
Values may be sent and summed in bfloat16 or wider, within the bound.
A program may use at most 64 MiB of HBM per device.

```python
import math
import jax
import jax.numpy as jnp
from jax import lax

D = 2560
QR = 768
MB = 2
STEP = 10
KVA = 288
GAINS = 1024
NF = 16


def scaled_grad(key, rows, cols):
    keys = jax.random.split(key, 3)
    spread = 4.0 / math.sqrt(2.0 * NF)
    row_scale = jnp.exp(jax.random.uniform(keys[0], (rows, 1), jnp.float32) * math.log(10.0))
    col_scale = jnp.exp(jax.random.uniform(keys[1], (1, cols), jnp.float32) * math.log(10.0))
    position = jnp.arange(rows, dtype=jnp.float32)
    ramp = jnp.sqrt(1.0 + 2.0 * position / rows)[:, None]
    owner = jnp.arange(rows, dtype=jnp.int32) // (rows // NF)
    spike = jnp.where(owner[None, :] == jnp.arange(NF, dtype=jnp.int32)[:, None], 3.0, 1.0).astype(jnp.float32)
    noise = jax.random.normal(keys[2], (MB, NF, rows, cols), jnp.float32)
    values = spread * noise * (row_scale * col_scale * ramp) * spike[None, :, :, None]
    return values.astype(jnp.bfloat16)


def draw_grad_query(key, part):
    return scaled_grad(jax.random.fold_in(key, 11), D, QR)


def draw_grad_latent(key, part):
    return scaled_grad(jax.random.fold_in(key, 12), D, KVA)


def draw_grad_gains(key, part):
    return scaled_grad(jax.random.fold_in(key, 13), GAINS, 1)[..., 0]


def level_of(key, dims, shards, low, top_value):
    level, own = 1.0, jax.random.fold_in(key, 6)
    for dim, parts in shards:
        steps = jnp.exp(jax.random.uniform(jax.random.fold_in(own, dim), (parts,), jnp.float32, low / len(shards), top_value / len(shards)))
        level = level * jnp.repeat(steps, dims[dim] // parts).reshape([-1 if axis == dim else 1 for axis in range(len(dims))])
    return level


def normal_values(key, extent, scale, bound, cuts=(), held_as=jnp.bfloat16):
    level = level_of(key, extent, cuts, -0.22, 0.18) if cuts else 1.0
    result = jax.random.normal(key, extent, jnp.float32) * scale * level
    return jnp.minimum(jnp.maximum(result, -bound), bound).astype(held_as)


def setup_inputs(seed: int = 0) -> dict:
    seeds = jax.random.split(jax.random.key(seed), 13)
    return {
        "grad_query": draw_grad_query(jax.random.fold_in(seeds[12], 71), 0),
        "grad_latent": draw_grad_latent(jax.random.fold_in(seeds[12], 71), 0),
        "grad_gains": draw_grad_gains(jax.random.fold_in(seeds[12], 71), 0),
        "param_query": normal_values(seeds[3], (D, QR), 0.02, 0.125, ((0, 16), (1, 2)), jnp.float32),
        "param_latent": normal_values(seeds[4], (D, KVA), 0.02, 0.125, ((0, 16), (1, 2)), jnp.float32),
        "param_gains": normal_values(seeds[5], (GAINS,), 0.02, 0.125, ((0, 16),), jnp.float32),
        "first_query": normal_values(seeds[6], (D, QR), 0.5, 4.0, ((0, 16), (1, 2)), jnp.float32),
        "first_latent": normal_values(seeds[7], (D, KVA), 0.5, 4.0, ((0, 16), (1, 2)), jnp.float32),
        "first_gains": normal_values(seeds[8], (GAINS,), 0.5, 4.0, ((0, 16),), jnp.float32),
        "second_query": jnp.clip(jnp.exp(math.log(2.0) - 3.6888794 * jax.random.uniform(seeds[9], (D, QR), jnp.float32) ** level_of(seeds[9], (D, QR), ((0, 16), (1, 2)), -0.2, 0.2)), 0.05, 2.0),
        "second_latent": jnp.clip(jnp.exp(math.log(2.0) - 3.6888794 * jax.random.uniform(seeds[10], (D, KVA), jnp.float32) ** level_of(seeds[10], (D, KVA), ((0, 16), (1, 2)), -0.2, 0.2)), 0.05, 2.0),
        "second_gains": jnp.clip(jnp.exp(math.log(2.0) - 3.6888794 * jax.random.uniform(seeds[11], (GAINS,), jnp.float32) ** level_of(seeds[11], (GAINS,), ((0, 16),), -0.2, 0.2)), 0.05, 2.0),
    }


beta_first = 0.9
beta_second = 0.95
rate = 0.01

def adamw(gradient, weights, first, second, factor, decay):
    scaled = factor * gradient
    first_new = beta_first * first + (1.0 - beta_first) * scaled
    second_new = beta_second * second + (1.0 - beta_second) * scaled * scaled
    ratio = first_new / (1.0 - beta_first ** STEP) / (jnp.sqrt(second_new / (1.0 - beta_second ** STEP)) + 1e-08)
    weights_new = weights - rate * (ratio + decay * weights)
    return (weights_new, first_new, second_new)

def reference(grad_query, grad_latent, grad_gains, param_query, param_latent, param_gains, first_query, first_latent, first_gains, second_query, second_latent, second_gains):
    sum_query = 0.5 * lax.optimization_barrier(jnp.sum(grad_query, axis=(0, 1), dtype=jnp.float32))
    sum_latent = 0.5 * lax.optimization_barrier(jnp.sum(grad_latent, axis=(0, 1), dtype=jnp.float32))
    sum_gains = 0.5 * lax.optimization_barrier(jnp.sum(grad_gains, axis=(0, 1), dtype=jnp.float32))
    squares = jnp.sum(sum_query * sum_query) + jnp.sum(sum_latent * sum_latent) + jnp.sum(sum_gains * sum_gains)
    count = D * (QR + KVA) + GAINS
    rms_value = jnp.sqrt(squares / count + 1e-06)
    factor = jnp.minimum(jnp.float32(1.0), 1.0 / rms_value)
    new_query, next_first_query, next_second_query = adamw(sum_query, param_query, first_query, second_query, factor, 0.1)
    new_latent, next_first_latent, next_second_latent = adamw(sum_latent, param_latent, first_latent, second_latent, factor, 0.1)
    new_gains, next_first_gains, next_second_gains = adamw(sum_gains, param_gains, first_gains, second_gains, factor, 0.0)
    return (new_query, new_latent, new_gains, next_first_query, next_first_latent, next_first_gains, next_second_query, next_second_latent, next_second_gains, new_query.astype(jnp.bfloat16), new_latent.astype(jnp.bfloat16), new_gains.astype(jnp.bfloat16))
```

```python
import functools

import jax
import jax.numpy as jnp
from jax import lax
from jax.experimental import pallas as pl
from jax.experimental.pallas import tpu as pltpu
from jax.sharding import PartitionSpec as P

STEP = 10

beta_first = 0.9
beta_second = 0.95
rate = 0.01

LANES = 128
MESH = pl.DeviceIdType.MESH
f32 = jnp.float32
bf16 = jnp.bfloat16


class Plan:
    def __init__(self, n, tp, mb, own_rows, wq, wl, gains):
        self.n, self.tp, self.mb, self.own_rows = n, tp, mb, own_rows
        self.m = n // 2
        self.bits = self.m.bit_length() - 1
        self.rp = -(-own_rows // 16) * 16
        self.wq, self.wl, self.gn = wq, wl, gains // n
        self.nq, self.nl, self.left = wq // LANES, wl // LANES, wl % LANES
        self.slots = LANES // self.left
        self.groups = self.rp // 16
        self.main = self.rp * (self.nq + self.nl)
        self.grow = self.main + 16 * (self.groups // self.slots)
        self.rows = self.grow + 16
        self.glane = 64
        assert wq % LANES == 0 and LANES % self.left == 0 and self.gn <= 64
        assert self.groups % self.slots * self.left <= self.glane
        assert 2 << self.bits == n
        self.cut = int(self.rows * 0.5) // 16 * 16
        self.halves = ((0, self.cut), (self.cut, self.rows - self.cut))
        first = list(range(self.bits))
        second = first[1:2] + first[:1] + first[2:]
        self.orders = (first, second)

    def leftover(self):
        for g in range(self.groups):
            yield self.main + 16 * (g // self.slots), self.left * (g % self.slots), 16 * g

    def slots_after(self, half, step):
        done = self.orders[half][: step + 1]
        return [d for d in range(self.m) if all(not d >> k & 1 for k in done)]

    def message(self, half, step, slot):
        base = half * (self.m - 1)
        for s in range(step):
            base += len(self.slots_after(half, s))
        return base + self.slots_after(half, step).index(slot)


def kernel(plan, count, *refs):
    (gq, gl, gg, pq, pl_, pg, fq, fl, fg, sq, sl, sg,
     nq, nl, ng, mq, ml, mg, vq, vl, vg, tq, tl, tg,
     own_q, own_l, in_q, in_l, in_g, gsum, acc, rbuf, total, stage, norm, ag, agc, tgs,
     cq_s, cq_r, cl_s, cl_r, cg_s, cg_r, oq, ol, rs_s, rs_r, no_s, no_r, ag_s, ag_r, ac_s, ac_r) = refs
    n, m, mb, tp, rp = plan.n, plan.m, plan.mb, plan.tp, plan.rp
    everyone = n * tp
    f, t = lax.axis_index("fsdp"), lax.axis_index("tp")
    core, up = f % 2, f // 2
    me = f * tp + t

    def flip(value, d):
        for k in range(plan.bits):
            if d >> k & 1:
                value = value + (1 << k) * (1 - 2 * (value // (1 << k) % 2))
        return value

    sibling = {"fsdp": f + 1 - 2 * core, "tp": t}

    def partner(k):
        return {"fsdp": 2 * flip(up, 1 << k) + core, "tp": t}

    def peer(i):
        other = (me + i) % everyone
        return {"fsdp": other // tp, "tp": other % tp}

    def mine(d):
        return 2 * flip(up, d) + core

    def theirs(d):
        return 2 * flip(up, d) + 1 - core

    def remote(src, dst, send, recv, to):
        return pltpu.make_async_remote_copy(
            src_ref=src, dst_ref=dst, send_sem=send, recv_sem=recv, device_id=to, device_id_type=MESH
        )

    order = sorted(range(1, m), key=lambda d: (not all(d >> o[0] & 1 for o in plan.orders),
                                               not any(d >> o[0] & 1 for o in plan.orders), d)) + [0]
    local_copies = []
    for d in order:
        a = pltpu.make_async_copy(gq.at[:, mine(d)], own_q.at[d], oq.at[d])
        b = pltpu.make_async_copy(gl.at[:, mine(d)], own_l.at[d], ol.at[d])
        a.start()
        b.start()
        local_copies.append((a, b))

    barrier = pltpu.get_barrier_semaphore()

    @pl.loop(1, everyone)
    def _(i):
        pl.semaphore_signal(barrier, inc=1, device_id=peer(i), device_id_type=MESH)

    pl.semaphore_wait(barrier, everyone - 1)

    gain_copy = remote(gg, in_g, cg_s.at[0], cg_r.at[0], sibling)
    gain_copy.start()
    core_copies = []
    for d in order:
        a = remote(gq.at[:, theirs(d)], in_q.at[d], cq_s.at[d], cq_r.at[d], sibling)
        b = remote(gl.at[:, theirs(d)], in_l.at[d], cl_s.at[d], cl_r.at[d], sibling)
        a.start()
        b.start()
        core_copies.append((a, b))

    def rs_copy(half, step, d):
        k = plan.orders[half][step]
        slot = d ^ (1 << k)
        index = plan.message(half, step, slot)
        lo, size = plan.halves[half]
        return remote(
            acc.at[d, pl.ds(lo, size)],
            rbuf.at[index, pl.ds(0, size)],
            rs_s.at[index],
            rs_r.at[index],
            partner(k),
        )

    def gather_sum(refs_, d, lo, hi):
        value = None
        for ref in refs_:
            for i in range(mb):
                term = ref[d, i, :, lo:hi].astype(f32)
                value = term if value is None else value + term
        return value

    gain_copy.wait()
    total_gains = None
    for ref in (gg, in_g):
        for i in range(mb):
            term = ref[i].astype(f32)
            total_gains = term if total_gains is None else total_gains + term
    gsum[...] = total_gains

    for place, d in enumerate(order):
        for copy in local_copies[place]:
            copy.wait()
        for copy in core_copies[place]:
            copy.wait()
        for j in range(plan.nq):
            acc[d, rp * j : rp * (j + 1)] = gather_sum((own_q, in_q), d, LANES * j, LANES * (j + 1))
        for j in range(plan.nl):
            lo = rp * (plan.nq + j)
            acc[d, lo : lo + rp] = gather_sum((own_l, in_l), d, LANES * j, LANES * (j + 1))
        acc[d, plan.main : plan.rows] = jnp.zeros((plan.rows - plan.main, LANES), f32)
        last = gather_sum((own_l, in_l), d, LANES * plan.nl, plan.wl)
        for row, lane, source in plan.leftover():
            acc[d, row : row + 16, lane : lane + plan.left] = last[source : source + 16]
        acc[d, plan.grow : plan.grow + 1, plan.glane : plan.glane + plan.gn] = gsum[pl.ds(mine(d), 1), :]
        for half in range(2):
            if d >> plan.orders[half][0] & 1:
                rs_copy(half, 0, d).start()

    def add_arrived(half, step, d):
        index = plan.message(half, step, d)
        lo, size = plan.halves[half]
        rs_copy(half, step, d ^ (1 << plan.orders[half][step])).wait_recv()
        acc[d, lo : lo + size] += rbuf[index, 0:size]

    for step in range(1, plan.bits):
        for half in range(2):
            k = plan.orders[half][step]
            for d in plan.slots_after(half, step - 1):
                if d >> k & 1:
                    for earlier in range(step):
                        add_arrived(half, earlier, d)
                    rs_copy(half, step, d).start()
    for step in range(plan.bits):
        for half in range(2):
            add_arrived(half, step, 0)

    summed = 0.5 * acc[0]
    total[...] = summed
    tail = summed[plan.main :]
    is_gain = (lax.broadcasted_iota(jnp.int32, tail.shape, 0) >= plan.grow - plan.main) & (
        lax.broadcasted_iota(jnp.int32, tail.shape, 1) >= plan.glane
    )
    tail_squares = jnp.where(is_gain, 1.0 / tp, 1.0) * tail * tail
    head = summed[: plan.main]
    squares = jnp.sum((head * head).reshape(-1, 8, LANES), axis=0)
    norm[0] = squares + jnp.sum(tail_squares.reshape(-1, 8, LANES), axis=0)

    def norm_copy(i):
        return remote(norm.at[0], norm.at[i], no_s.at[i], no_r.at[i], peer(i))

    @pl.loop(1, everyone)
    def _(i):
        norm_copy(i).start()

    @pl.loop(1, everyone)
    def _(i):
        norm_copy(i).wait()

    sum_squares = jnp.sum(jnp.sum(norm[...], axis=0), keepdims=True)
    rms = jnp.sqrt(jnp.broadcast_to(sum_squares, (1, LANES)) / count + 1e-06)
    factor = jnp.minimum(f32(1.0), 1.0 / rms)

    def update(gradient, p, first, second, decay):
        scaled = factor[:, : gradient.shape[1]] * gradient
        first_new = beta_first * first + (1.0 - beta_first) * scaled
        second_new = beta_second * second + (1.0 - beta_second) * scaled * scaled
        ratio = (first_new / (1.0 - beta_first**STEP)) / (
            jnp.sqrt(second_new / (1.0 - beta_second**STEP)) + 1e-08
        )
        return p - rate * (ratio + decay * p), first_new, second_new

    for j in range(plan.nq + plan.nl):
        params = (pq, fq, sq) if j < plan.nq else (pl_, fl, sl)
        outs = (nq, mq, vq) if j < plan.nq else (nl, ml, vl)
        lo = LANES * (j if j < plan.nq else j - plan.nq)
        values = update(total[rp * j : rp * (j + 1)], *(ref[:, lo : lo + LANES] for ref in params), 0.1)
        for ref, value in zip(outs, values):
            ref[:, lo : lo + LANES] = value
        ag[0, rp * j : rp * (j + 1)] = values[0].astype(bf16)
    stage[...] = jnp.zeros(stage.shape, f32)
    for row, lane, source in plan.leftover():
        at = (pl.ds(source, 16), pl.ds(LANES * plan.nl, plan.left))
        values = update(total[row : row + 16, lane : lane + plan.left], pl_[at], fl[at], sl[at], 0.1)
        for ref, value in zip((nl, ml, vl), values):
            ref[at] = value
        stage[row - plan.main : row - plan.main + 16, lane : lane + plan.left] = values[0]
    gain_lanes = (slice(plan.grow, plan.grow + 1), slice(plan.glane, plan.glane + plan.gn))
    values = update(total[gain_lanes], pg[...], fg[...], sg[...], 0.0)
    for ref, value in zip((ng, mg, vg), values):
        ref[...] = value
    stage[plan.grow - plan.main : plan.grow - plan.main + 1, gain_lanes[1]] = values[0]
    ag[0, plan.main : plan.rows] = stage[...].astype(bf16)

    def ag_copy(half, step, d):
        k = plan.orders[half][step]
        source = d ^ (1 << k)
        index = plan.message(half, step, source if d >> k & 1 else d)
        lo, size = plan.halves[half]
        rows = pl.ds(lo, size)
        return remote(ag.at[d, rows], ag.at[source, rows], ag_s.at[index], ag_r.at[index], partner(k))

    def across(half, d):
        lo, size = plan.halves[half]
        rows = pl.ds(lo, size)
        index = half * m + d
        return remote(ag.at[d, rows], agc.at[d, rows], ac_s.at[index], ac_r.at[index], sibling)

    def arrived(half, step, d):
        for later in reversed(range(step)):
            ag_copy(half, later, d).start()
        across(half, d).start()

    def write(ref, d, block):
        for j in range(plan.nq):
            tq[block, :, LANES * j : LANES * (j + 1)] = ref[d, rp * j : rp * (j + 1)]
        for j in range(plan.nl):
            lo = rp * (plan.nq + j)
            tl[block, :, LANES * j : LANES * (j + 1)] = ref[d, lo : lo + rp]
        for row, lane, source in plan.leftover():
            tl[block, source : source + 16, LANES * plan.nl : plan.wl] = ref[
                d, row : row + 16, lane : lane + plan.left
            ]
        gains = ref[d, plan.grow : plan.grow + 16].astype(f32)
        tgs[pl.ds(block, 1), :] = gains[0:1, plan.glane : plan.glane + plan.gn]

    for half in range(2):
        arrived(half, plan.bits, 0)
    write(ag, 0, mine(0))
    for step in reversed(range(plan.bits)):
        for half in range(2):
            k = plan.orders[half][step]
            for d in plan.slots_after(half, step):
                new = d | (1 << k)
                ag_copy(half, step, d).wait_recv()
                arrived(half, step, new)
    for d in range(1, m):
        write(ag, d, mine(d))
    for d in range(m):
        for half in range(2):
            across(half, d).wait_recv()
        write(agc, d, theirs(d))
    tg[...] = tgs[...].astype(bf16)

    for half in range(2):
        for step in range(plan.bits):
            k = plan.orders[half][step]
            for d in plan.slots_after(half, step):
                rs_copy(half, step, d | (1 << k)).wait_send()
                ag_copy(half, step, d).wait_send()
        for d in range(m):
            across(half, d).wait_send()


def local(grad_query, grad_latent, grad_gains, *state):
    n, tp = lax.axis_size("fsdp"), lax.axis_size("tp")
    mb, _, depth, wq = grad_query.shape
    wl, gains = grad_latent.shape[3], grad_gains.shape[2]
    plan = Plan(n, tp, mb, depth // n, wq, wl, gains)
    count = depth * (wq + wl) * tp + gains
    extra = plan.rp - plan.own_rows

    def blocks(x):
        x = x.reshape(mb, n, plan.own_rows, x.shape[3])
        return jnp.pad(x, ((0, 0), (0, 0), (0, extra), (0, 0))) if extra else x

    def own(x):
        if x.ndim == 1:
            return x.reshape(1, plan.gn)
        return jnp.pad(x, ((0, extra), (0, 0))) if extra else x

    state = [own(x) for x in state]
    m, rp = plan.m, plan.rp
    vmem = pl.BlockSpec(memory_space=pltpu.VMEM)
    anywhere = pl.BlockSpec(memory_space=pl.ANY)
    shapes = [(rp, wq), (rp, wl), (1, plan.gn)] * 3
    outs = pl.pallas_call(
        functools.partial(kernel, plan, count),
        out_shape=[jax.ShapeDtypeStruct(s, f32) for s in shapes]
        + [
            jax.ShapeDtypeStruct((n, rp, wq), bf16),
            jax.ShapeDtypeStruct((n, rp, wl), bf16),
            jax.ShapeDtypeStruct((n, plan.gn), bf16),
        ],
        in_specs=[anywhere, anywhere] + [vmem] * 10,
        out_specs=[vmem] * 12,
        scratch_shapes=[
            pltpu.VMEM((m, mb, rp, wq), bf16),
            pltpu.VMEM((m, mb, rp, wl), bf16),
            pltpu.VMEM((m, mb, rp, wq), bf16),
            pltpu.VMEM((m, mb, rp, wl), bf16),
            pltpu.VMEM((mb, n, plan.gn), bf16),
            pltpu.VMEM((n, plan.gn), f32),
            pltpu.VMEM((m, plan.rows, LANES), f32),
            pltpu.VMEM((2 * (m - 1), max(s for _, s in plan.halves), LANES), f32),
            pltpu.VMEM((plan.rows, LANES), f32),
            pltpu.VMEM((plan.rows - plan.main, LANES), f32),
            pltpu.VMEM((n * tp, 8, LANES), f32),
            pltpu.VMEM((m, plan.rows, LANES), bf16),
            pltpu.VMEM((m, plan.rows, LANES), bf16),
            pltpu.VMEM((n, plan.gn), f32),
        ]
        + [
            pltpu.SemaphoreType.DMA((k,))
            for k in [m] * 4 + [1] * 2 + [m] * 2 + [2 * (m - 1)] * 2 + [n * tp] * 2 + [2 * (m - 1)] * 2 + [2 * m] * 2
        ],
        compiler_params=pltpu.CompilerParams(
            collective_id=0, has_side_effects=True, vmem_limit_bytes=52 * 1024 * 1024
        ),
    )(blocks(grad_query), blocks(grad_latent), grad_gains.reshape(mb, n, plan.gn), *state)
    result = []
    for x in outs[:9]:
        if x.shape[0] == 1:
            result.append(x.reshape(plan.gn))
        else:
            result.append(x[: plan.own_rows] if extra else x)
    for x in outs[9:11]:
        result.append(x[:, : plan.own_rows].reshape(depth, x.shape[2]))
    result.append(outs[11].reshape(gains))
    return tuple(result)


def solution(mesh):
    shards = (P("fsdp", "tp"), P("fsdp", "tp"), P("fsdp"))
    in_specs = (P(None, "fsdp", None, "tp"), P(None, "fsdp", None, "tp"), P(None, "fsdp", None)) + shards * 3
    out_specs = shards * 3 + (P(None, "tp"), P(None, "tp"), P())
    return jax.shard_map(local, mesh=mesh, in_specs=in_specs, out_specs=out_specs, check_vma=False)
```

```python
import functools
import math

import jax
import jax.numpy as jnp
from jax import lax
from jax.experimental import pallas as pl
from jax.experimental.pallas import tpu as pltpu
from jax.sharding import PartitionSpec as P

STEP = 10

beta_first = 0.9
beta_second = 0.95
rate = 0.01

LANES = 128
MESH = pl.DeviceIdType.MESH
f32 = jnp.float32
bf16 = jnp.bfloat16


class Plan:
    def __init__(self, n, tp, mb, own_rows, wq, wl, gains, share=0.5):
        self.n, self.tp, self.mb, self.own_rows = n, tp, mb, own_rows
        self.depth = n * own_rows
        self.m = n // 2
        self.bits = self.m.bit_length() - 1
        self.rp = -(-own_rows // 16) * 16
        self.wq, self.wl, self.gn = wq, wl, gains // n
        self.nq, self.nl, self.left = wq // LANES, own_rows // LANES, own_rows % LANES
        self.slot = 1 << max(0, self.left - 1).bit_length()
        self.slots = LANES // self.slot
        self.groups = wl // 16
        self.main = self.rp * self.nq + wl * self.nl
        self.grow = self.main + 16 * (self.groups // self.slots)
        self.rows = self.grow + 16
        self.glane = 64
        self.per = LANES // self.gn
        assert wq % LANES == 0 and wl % 16 == 0 and self.left and self.gn <= 64
        assert LANES % self.gn == 0 and self.groups % self.slots * self.slot <= self.glane
        assert 2 << self.bits == n
        self.cut = int(self.rows * share) // 16 * 16
        self.halves = ((0, self.cut), (self.cut, self.rows - self.cut))
        first = list(range(self.bits))
        second = first[1:2] + first[:1] + first[2:]
        self.orders = (first, second)

    def leftover(self):
        for g in range(self.groups):
            yield self.main + 16 * (g // self.slots), self.slot * (g % self.slots), 16 * g

    def window(self, block):
        tile = self.own_rows * block // LANES
        if self.own_rows * (self.n - 1) // LANES > self.depth // LANES - 2:
            tile = jnp.minimum(tile, self.depth // LANES - 2)
        return pl.ds(pl.multiple_of(LANES * tile, LANES), 2 * LANES), self.own_rows * block - LANES * tile

    def slots_after(self, half, step):
        done = self.orders[half][: step + 1]
        return [d for d in range(self.m) if all(not d >> k & 1 for k in done)]

    def message(self, half, step, slot):
        base = half * (self.m - 1)
        for s in range(step):
            base += len(self.slots_after(half, s))
        return base + self.slots_after(half, step).index(slot)


def kernel(plan, count, *refs):
    (gq, gl, gg, pq, pl_, pg, fq, fl, fg, sq, sl, sg,
     nq, nl, ng, mq, ml, mg, vq, vl, vg, tq, tl, tg,
     in_q, in_l, in_g, gsum, acc, rbuf, total, stage, norm, ag, agc, tgs, tls, lat,
     cq_s, cq_r, cl_s, cl_r, cg_s, cg_r, rs_s, rs_r, no_s, no_r, ag_s, ag_r, ac_s, ac_r) = refs
    n, m, mb, tp, rp = plan.n, plan.m, plan.mb, plan.tp, plan.rp
    everyone, wl = n * tp, plan.wl
    f, t = lax.axis_index("fsdp"), lax.axis_index("tp")
    core, up = f % 2, f // 2
    me = f * tp + t

    def flip(value, d):
        for k in range(plan.bits):
            if d >> k & 1:
                value = value + (1 << k) * (1 - 2 * (value // (1 << k) % 2))
        return value

    sibling = {"fsdp": f + 1 - 2 * core, "tp": t}

    def partner(k):
        return {"fsdp": 2 * flip(up, 1 << k) + core, "tp": t}

    def peer(i):
        other = (me + i) % everyone
        return {"fsdp": other // tp, "tp": other % tp}

    def mine(d):
        return 2 * flip(up, d) + core

    def theirs(d):
        return 2 * flip(up, d) + 1 - core

    def gain_window(block):
        return pl.ds(pl.multiple_of(LANES * (block // plan.per), LANES), LANES), plan.gn * (block % plan.per)

    def remote(src, dst, send, recv, to):
        return pltpu.make_async_remote_copy(
            src_ref=src, dst_ref=dst, send_sem=send, recv_sem=recv, device_id=to, device_id_type=MESH
        )

    order = sorted(range(1, m), key=lambda d: (not all(d >> o[0] & 1 for o in plan.orders),
                                               not any(d >> o[0] & 1 for o in plan.orders), d)) + [0]
    tls[...] = jnp.zeros(tls.shape, f32)
    tgs[...] = jnp.zeros(tgs.shape, f32)
    barrier = pltpu.get_barrier_semaphore()

    @pl.loop(1, everyone)
    def _(i):
        pl.semaphore_signal(barrier, inc=1, device_id=peer(i), device_id_type=MESH)

    pl.semaphore_wait(barrier, everyone - 1)

    gain_copy = remote(gg, in_g, cg_s.at[0], cg_r.at[0], sibling)
    gain_copy.start()
    core_copies = []
    for d in order:
        a = remote(gq.at[:, theirs(d)], in_q.at[d], cq_s.at[d], cq_r.at[d], sibling)
        b = remote(gl.at[:, :, plan.window(theirs(d))[0]], in_l.at[d], cl_s.at[d], cl_r.at[d], sibling)
        a.start()
        b.start()
        core_copies.append((a, b))

    def rs_copy(half, step, d):
        k = plan.orders[half][step]
        slot = d ^ (1 << k)
        index = plan.message(half, step, slot)
        lo, size = plan.halves[half]
        return remote(
            acc.at[d, pl.ds(lo, size)],
            rbuf.at[index, pl.ds(0, size)],
            rs_s.at[index],
            rs_r.at[index],
            partner(k),
        )

    def added(terms):
        value = None
        for term in terms:
            value = term.astype(f32) if value is None else value + term.astype(f32)
        return value

    gain_copy.wait()
    total_gains = added([ref[i] for ref in (gg, in_g) for i in range(mb)])
    gsum[...] = jnp.broadcast_to(total_gains, gsum.shape)

    for place, d in enumerate(order):
        for copy in core_copies[place]:
            copy.wait()
        for j in range(plan.nq):
            acc[d, rp * j : rp * (j + 1)] = added(
                [gq[i, mine(d), :, LANES * j : LANES * (j + 1)] for i in range(mb)]
                + [in_q[d, i, :, LANES * j : LANES * (j + 1)] for i in range(mb)]
            )
        acc[d, plan.main : plan.rows] = jnp.zeros((plan.rows - plan.main, LANES), f32)
        tile, start = plan.window(mine(d))
        latent = added([gl[i, :, tile] for i in range(mb)] + [in_l[d, i] for i in range(mb)])
        latent = pltpu.roll(latent, (2 * LANES - start) % (2 * LANES), 1)
        for j in range(plan.nl):
            lo = rp * plan.nq + wl * j
            acc[d, lo : lo + wl] = latent[:, LANES * j : LANES * (j + 1)]
        for row, lane, source in plan.leftover():
            acc[d, row : row + 16, lane : lane + plan.left] = latent[
                source : source + 16, LANES * plan.nl : LANES * plan.nl + plan.left
            ]
        tile, start = gain_window(mine(d))
        gains = pltpu.roll(gsum[:, tile], (plan.glane - start + LANES) % LANES, 1)
        acc[d, plan.grow : plan.grow + 1, plan.glane : plan.glane + plan.gn] = gains[
            0:1, plan.glane : plan.glane + plan.gn
        ]
        for half in range(2):
            if d >> plan.orders[half][0] & 1:
                rs_copy(half, 0, d).start()

    def add_arrived(half, step, d):
        index = plan.message(half, step, d)
        lo, size = plan.halves[half]
        rs_copy(half, step, d ^ (1 << plan.orders[half][step])).wait_recv()
        acc[d, lo : lo + size] += rbuf[index, 0:size]

    for step in range(1, plan.bits):
        for half in range(2):
            k = plan.orders[half][step]
            for d in plan.slots_after(half, step - 1):
                if d >> k & 1:
                    for earlier in range(step):
                        add_arrived(half, earlier, d)
                    rs_copy(half, step, d).start()
    for step in range(plan.bits):
        for half in range(2):
            add_arrived(half, step, 0)

    summed = 0.5 * acc[0]
    total[...] = summed
    tail = summed[plan.main :]
    is_gain = (lax.broadcasted_iota(jnp.int32, tail.shape, 0) >= plan.grow - plan.main) & (
        lax.broadcasted_iota(jnp.int32, tail.shape, 1) >= plan.glane
    )
    tail_squares = jnp.where(is_gain, 1.0 / tp, 1.0) * tail * tail
    head = summed[: plan.main]
    squares = jnp.sum((head * head).reshape(-1, 8, LANES), axis=0)
    norm[0] = squares + jnp.sum(tail_squares.reshape(-1, 8, LANES), axis=0)

    def norm_copy(i):
        return remote(norm.at[0], norm.at[i], no_s.at[i], no_r.at[i], peer(i))

    @pl.loop(1, everyone)
    def _(i):
        norm_copy(i).start()

    @pl.loop(1, everyone)
    def _(i):
        norm_copy(i).wait()

    sum_squares = jnp.sum(jnp.sum(norm[...], axis=0), keepdims=True)
    rms = jnp.sqrt(jnp.broadcast_to(sum_squares, (1, LANES)) / count + 1e-06)
    factor = jnp.minimum(f32(1.0), 1.0 / rms)

    def update(gradient, p, first, second, decay):
        scaled = factor[:, : gradient.shape[1]] * gradient
        first_new = beta_first * first + (1.0 - beta_first) * scaled
        second_new = beta_second * second + (1.0 - beta_second) * scaled * scaled
        ratio = (first_new / (1.0 - beta_first**STEP)) / (
            jnp.sqrt(second_new / (1.0 - beta_second**STEP)) + 1e-08
        )
        return p - rate * (ratio + decay * p), first_new, second_new

    for j in range(plan.nq + plan.nl):
        query = j < plan.nq
        params = (pq, fq, sq) if query else (pl_, fl, sl)
        outs = (nq, mq, vq) if query else (nl, ml, vl)
        lane = LANES * (j if query else j - plan.nq)
        lo, size = (rp * j, rp) if query else (rp * plan.nq + wl * (j - plan.nq), wl)
        values = update(total[lo : lo + size], *(ref[:, lane : lane + LANES] for ref in params), 0.1)
        for ref, value in zip(outs, values):
            ref[:, lane : lane + LANES] = value
        ag[0, lo : lo + size] = values[0].astype(bf16)
    stage[...] = jnp.zeros(stage.shape, f32)
    for row, lane, source in plan.leftover():
        at = (pl.ds(source, 16), pl.ds(LANES * plan.nl, plan.left))
        values = update(total[row : row + 16, lane : lane + plan.left], pl_[at], fl[at], sl[at], 0.1)
        for ref, value in zip((nl, ml, vl), values):
            ref[at] = value
        stage[row - plan.main : row - plan.main + 16, lane : lane + plan.left] = values[0]
    gain_lanes = (slice(plan.grow, plan.grow + 1), slice(plan.glane, plan.glane + plan.gn))
    values = update(total[gain_lanes], pg[...], fg[...], sg[...], 0.0)
    for ref, value in zip((ng, mg, vg), values):
        ref[...] = value
    stage[plan.grow - plan.main : plan.grow - plan.main + 1, gain_lanes[1]] = values[0]
    ag[0, plan.main : plan.rows] = stage[...].astype(bf16)

    def ag_copy(half, step, d):
        k = plan.orders[half][step]
        source = d ^ (1 << k)
        index = plan.message(half, step, source if d >> k & 1 else d)
        lo, size = plan.halves[half]
        rows = pl.ds(lo, size)
        return remote(ag.at[d, rows], ag.at[source, rows], ag_s.at[index], ag_r.at[index], partner(k))

    def across(half, d):
        lo, size = plan.halves[half]
        rows = pl.ds(lo, size)
        index = half * m + d
        return remote(ag.at[d, rows], agc.at[d, rows], ac_s.at[index], ac_r.at[index], sibling)

    def arrived(half, step, d):
        for later in reversed(range(step)):
            ag_copy(half, later, d).start()
        across(half, d).start()

    def write(ref, d, block):
        for j in range(plan.nq):
            tq[block, :, LANES * j : LANES * (j + 1)] = ref[d, rp * j : rp * (j + 1)]
        for j in range(plan.nl):
            lo = rp * plan.nq + wl * j
            lat[:, LANES * j : LANES * (j + 1)] = ref[d, lo : lo + wl].astype(f32)
        last = ref[d, plan.main : plan.rows].astype(f32)
        for row, lane, source in plan.leftover():
            row -= plan.main
            lat[source : source + 16, LANES * plan.nl : LANES * plan.nl + plan.left] = last[
                row : row + 16, lane : lane + plan.left
            ]
        tile, start = plan.window(block)
        lanes = lax.broadcasted_iota(jnp.int32, lat.shape, 1)
        inside = (lanes >= start) & (lanes < start + plan.own_rows)
        tls[:, tile] = jnp.where(inside, pltpu.roll(lat[...], start, 1), tls[:, tile])
        tile, start = gain_window(block)
        row = plan.grow - plan.main
        gains = pltpu.roll(last[row : row + 8], (start - plan.glane + LANES) % LANES, 1)
        lanes = lax.broadcasted_iota(jnp.int32, gains.shape, 1)
        tgs[:, tile] = jnp.where((lanes >= start) & (lanes < start + plan.gn), gains, tgs[:, tile])

    for half in range(2):
        arrived(half, plan.bits, 0)
    write(ag, 0, mine(0))
    for step in reversed(range(plan.bits)):
        for half in range(2):
            k = plan.orders[half][step]
            for d in plan.slots_after(half, step):
                new = d | (1 << k)
                ag_copy(half, step, d).wait_recv()
                arrived(half, step, new)
    for d in range(1, m):
        write(ag, d, mine(d))
    for d in range(m):
        for half in range(2):
            across(half, d).wait_recv()
        write(agc, d, theirs(d))
    tl[...] = tls[...].astype(bf16)
    tg[...] = tgs[0:1].astype(bf16)

    for half in range(2):
        for step in range(plan.bits):
            k = plan.orders[half][step]
            for d in plan.slots_after(half, step):
                rs_copy(half, step, d | (1 << k)).wait_send()
                ag_copy(half, step, d).wait_send()
        for d in range(m):
            across(half, d).wait_send()


def hand_over(*refs):
    count = len(refs) // 2
    sems = refs[-1]
    copies = [pltpu.make_async_copy(refs[i], refs[count + i], sems.at[i]) for i in range(count)]
    for copy in copies:
        copy.start()
    for copy in copies:
        copy.wait()


def local(grad_query, grad_latent, grad_gains, *state):
    n, tp = lax.axis_size("fsdp"), lax.axis_size("tp")
    mb, _, depth, wq = grad_query.shape
    wl, gains = grad_latent.shape[3], grad_gains.shape[2]
    plan = Plan(n, tp, mb, depth // n, wq, wl, gains)
    count = depth * (wq + wl) * tp + gains
    extra = plan.rp - plan.own_rows

    def pad(x):
        return jnp.pad(x, [(0, 0)] * (x.ndim - 2) + [(0, extra), (0, 0)]) if extra else x

    query = pad(grad_query.reshape(mb, n, plan.own_rows, wq))
    latent = jnp.swapaxes(grad_latent[:, 0], 1, 2)
    kept = []
    for i in range(3):
        kept += [pad(state[3 * i]), state[3 * i + 1].T, state[3 * i + 2].reshape(1, plan.gn)]
    m, rp = plan.m, plan.rp
    vmem = pl.BlockSpec(memory_space=pltpu.VMEM)
    hbm = pl.BlockSpec(memory_space=pltpu.HBM)
    out_shape = [
        jax.ShapeDtypeStruct(s, f32) for s in [(rp, wq), (wl, plan.own_rows), (1, plan.gn)] * 3
    ] + [jax.ShapeDtypeStruct(s, bf16) for s in [(n, rp, wq), (wl, depth), (1, gains)]]
    scratch = [
        pltpu.VMEM((m, mb, rp, wq), bf16),
        pltpu.VMEM((m, mb, wl, 2 * LANES), bf16),
        pltpu.VMEM((mb, 1, gains), bf16),
        pltpu.VMEM((8, gains), f32),
        pltpu.VMEM((m, plan.rows, LANES), f32),
        pltpu.VMEM((2 * (m - 1), max(s for _, s in plan.halves), LANES), f32),
        pltpu.VMEM((plan.rows, LANES), f32),
        pltpu.VMEM((plan.rows - plan.main, LANES), f32),
        pltpu.VMEM((n * tp, 8, LANES), f32),
        pltpu.VMEM((m, plan.rows, LANES), bf16),
        pltpu.VMEM((m, plan.rows, LANES), bf16),
        pltpu.VMEM((8, gains), f32),
        pltpu.VMEM((wl, depth), f32),
        pltpu.VMEM((wl, 2 * LANES), f32),
    ]
    planned = sum(math.prod(x.shape) * x.dtype.itemsize for x in scratch)
    outs = pl.pallas_call(
        functools.partial(kernel, plan, count),
        out_shape=out_shape,
        in_specs=[vmem] * 12,
        out_specs=[vmem] * 12,
        scratch_shapes=scratch
        + [
            pltpu.SemaphoreType.DMA((k,))
            for k in [m] * 4 + [1] * 2 + [2 * (m - 1)] * 2 + [n * tp] * 2 + [2 * (m - 1)] * 2 + [2 * m] * 2
        ],
        compiler_params=pltpu.CompilerParams(
            collective_id=0, has_side_effects=True, vmem_limit_bytes=planned + (14 << 20)
        ),
    )(query, latent, grad_gains, *kept)
    outs = pl.pallas_call(
        hand_over,
        out_shape=out_shape,
        in_specs=[vmem] * 12,
        out_specs=[hbm] * 12,
        scratch_shapes=[pltpu.SemaphoreType.DMA((12,))],
        compiler_params=pltpu.CompilerParams(vmem_limit_bytes=8 << 20),
    )(*outs)
    result = []
    for i in range(3):
        result += [outs[3 * i][: plan.own_rows], outs[3 * i + 1].T, outs[3 * i + 2].reshape(plan.gn)]
    result += [outs[9][:, : plan.own_rows].reshape(depth, wq), outs[10].T, outs[11].reshape(gains)]
    return tuple(result)


def solution(mesh):
    shards = (P("fsdp", "tp"), P("fsdp", "tp"), P("fsdp"))
    in_specs = (P(None, "fsdp", None, "tp"), P(None, "fsdp", None, "tp"), P(None, "fsdp", None)) + shards * 3
    out_specs = shards * 3 + (P(None, "tp"), P(None, "tp"), P())
    return jax.shard_map(local, mesh=mesh, in_specs=in_specs, out_specs=out_specs, check_vma=False)
```

```python
import functools
import math

import jax
import jax.numpy as jnp
from jax import lax
from jax.experimental import pallas as pl
from jax.experimental.pallas import tpu as pltpu
from jax.sharding import PartitionSpec as P

STEP = 10

beta_first = 0.9
beta_second = 0.95
rate = 0.01

LANES = 128
MESH = pl.DeviceIdType.MESH
f32 = jnp.float32
bf16 = jnp.bfloat16


class Plan:
    def __init__(self, n, tp, mb, own_rows, wq, wl, gains, share=0.5):
        self.n, self.tp, self.mb, self.own_rows = n, tp, mb, own_rows
        self.depth = n * own_rows
        self.m = n // 2
        self.bits = self.m.bit_length() - 1
        self.rp = -(-own_rows // 16) * 16
        self.wq, self.wl, self.gn = wq, wl, gains // n
        self.nq, self.nl, self.left = wq // LANES, own_rows // LANES, own_rows % LANES
        self.slot = 1 << max(0, self.left - 1).bit_length()
        self.slots = LANES // self.slot
        self.groups = wl // 16
        self.main = self.rp * self.nq + wl * self.nl
        self.grow = self.main + 16 * (self.groups // self.slots)
        self.rows = self.grow + 16
        self.glane = 64
        self.per = LANES // self.gn
        assert wq % LANES == 0 and wl % 16 == 0 and self.left and self.gn <= 64
        assert LANES % self.gn == 0 and self.groups % self.slots * self.slot <= self.glane
        assert 2 << self.bits == n
        self.cut = int(self.rows * share) // 16 * 16
        self.halves = ((0, self.cut), (self.cut, self.rows - self.cut))
        first = list(range(self.bits))
        second = first[1:2] + first[:1] + first[2:]
        self.orders = (first, second)

    def leftover(self):
        for g in range(self.groups):
            yield self.main + 16 * (g // self.slots), self.slot * (g % self.slots), 16 * g

    def window(self, block):
        tile = self.own_rows * block // LANES
        if self.own_rows * (self.n - 1) // LANES > self.depth // LANES - 2:
            tile = jnp.minimum(tile, self.depth // LANES - 2)
        return pl.ds(pl.multiple_of(LANES * tile, LANES), 2 * LANES), self.own_rows * block - LANES * tile

    def slots_after(self, half, step):
        done = self.orders[half][: step + 1]
        return [d for d in range(self.m) if all(not d >> k & 1 for k in done)]

    def message(self, half, step, slot):
        base = half * (self.m - 1)
        for s in range(step):
            base += len(self.slots_after(half, s))
        return base + self.slots_after(half, step).index(slot)


def kernel(plan, count, *refs):
    (gq, gl, gg, pq, pl_, pg, fq, fl, fg, sq, sl, sg,
     nq, nl, ng, mq, ml, mg, vq, vl, vg, tq, tl, tg,
     in_q, in_l, in_g, gsum, acc, rbuf, total, stage, norm, ag, agc, tgs, tls, lat,
     cq_s, cq_r, cl_s, cl_r, cg_s, cg_r, rs_s, rs_r, no_s, no_r, ag_s, ag_r, ac_s, ac_r) = refs
    n, m, mb, tp, rp = plan.n, plan.m, plan.mb, plan.tp, plan.rp
    everyone, wl = n * tp, plan.wl
    f, t = lax.axis_index("fsdp"), lax.axis_index("tp")
    core, up = f % 2, f // 2
    me = f * tp + t

    def flip(value, d):
        for k in range(plan.bits):
            if d >> k & 1:
                value = value + (1 << k) * (1 - 2 * (value // (1 << k) % 2))
        return value

    sibling = {"fsdp": f + 1 - 2 * core, "tp": t}

    def partner(k):
        return {"fsdp": 2 * flip(up, 1 << k) + core, "tp": t}

    def peer(i):
        other = (me + i) % everyone
        return {"fsdp": other // tp, "tp": other % tp}

    def mine(d):
        return 2 * flip(up, d) + core

    def theirs(d):
        return 2 * flip(up, d) + 1 - core

    def gain_window(block):
        return pl.ds(pl.multiple_of(LANES * (block // plan.per), LANES), LANES), plan.gn * (block % plan.per)

    def remote(src, dst, send, recv, to):
        return pltpu.make_async_remote_copy(
            src_ref=src, dst_ref=dst, send_sem=send, recv_sem=recv, device_id=to, device_id_type=MESH
        )

    order = sorted(range(1, m), key=lambda d: (not all(d >> o[0] & 1 for o in plan.orders),
                                               not any(d >> o[0] & 1 for o in plan.orders), d)) + [0]
    tls[...] = jnp.zeros(tls.shape, f32)
    tgs[...] = jnp.zeros(tgs.shape, f32)
    barrier = pltpu.get_barrier_semaphore()

    @pl.loop(1, everyone)
    def _(i):
        pl.semaphore_signal(barrier, inc=1, device_id=peer(i), device_id_type=MESH)

    pl.semaphore_wait(barrier, everyone - 1)

    gain_copy = remote(gg, in_g, cg_s.at[0], cg_r.at[0], sibling)
    gain_copy.start()
    core_copies = []
    for d in order:
        a = remote(gq.at[:, theirs(d)], in_q.at[d], cq_s.at[d], cq_r.at[d], sibling)
        b = remote(gl.at[:, :, plan.window(theirs(d))[0]], in_l.at[d], cl_s.at[d], cl_r.at[d], sibling)
        a.start()
        b.start()
        core_copies.append((a, b))

    def rs_copy(half, step, d):
        k = plan.orders[half][step]
        slot = d ^ (1 << k)
        index = plan.message(half, step, slot)
        lo, size = plan.halves[half]
        return remote(
            acc.at[d, pl.ds(lo, size)],
            rbuf.at[index, pl.ds(0, size)],
            rs_s.at[index],
            rs_r.at[index],
            partner(k),
        )

    def added(terms):
        value = None
        for term in terms:
            value = term.astype(f32) if value is None else value + term.astype(f32)
        return value

    gain_copy.wait()
    total_gains = added([ref[i] for ref in (gg, in_g) for i in range(mb)])
    gsum[...] = jnp.broadcast_to(total_gains, gsum.shape)

    for place, d in enumerate(order):
        for copy in core_copies[place]:
            copy.wait()
        for j in range(plan.nq):
            acc[d, rp * j : rp * (j + 1)] = added(
                [gq[i, mine(d), :, LANES * j : LANES * (j + 1)] for i in range(mb)]
                + [in_q[d, i, :, LANES * j : LANES * (j + 1)] for i in range(mb)]
            )
        acc[d, plan.main : plan.rows] = jnp.zeros((plan.rows - plan.main, LANES), f32)
        tile, start = plan.window(mine(d))
        latent = added([gl[i, :, tile] for i in range(mb)] + [in_l[d, i] for i in range(mb)])
        latent = pltpu.roll(latent, (2 * LANES - start) % (2 * LANES), 1)
        for j in range(plan.nl):
            lo = rp * plan.nq + wl * j
            acc[d, lo : lo + wl] = latent[:, LANES * j : LANES * (j + 1)]
        for row, lane, source in plan.leftover():
            acc[d, row : row + 16, lane : lane + plan.left] = latent[
                source : source + 16, LANES * plan.nl : LANES * plan.nl + plan.left
            ]
        tile, start = gain_window(mine(d))
        gains = pltpu.roll(gsum[:, tile], (plan.glane - start + LANES) % LANES, 1)
        acc[d, plan.grow : plan.grow + 1, plan.glane : plan.glane + plan.gn] = gains[
            0:1, plan.glane : plan.glane + plan.gn
        ]
        for half in range(2):
            if d >> plan.orders[half][0] & 1:
                rs_copy(half, 0, d).start()

    def add_arrived(half, step, d):
        index = plan.message(half, step, d)
        lo, size = plan.halves[half]
        rs_copy(half, step, d ^ (1 << plan.orders[half][step])).wait_recv()
        acc[d, lo : lo + size] += rbuf[index, 0:size]

    for step in range(1, plan.bits):
        for half in range(2):
            k = plan.orders[half][step]
            for d in plan.slots_after(half, step - 1):
                if d >> k & 1:
                    for earlier in range(step):
                        add_arrived(half, earlier, d)
                    rs_copy(half, step, d).start()
    for step in range(plan.bits):
        for half in range(2):
            add_arrived(half, step, 0)

    summed = 0.5 * acc[0]
    total[...] = summed
    tail = summed[plan.main :]
    is_gain = (lax.broadcasted_iota(jnp.int32, tail.shape, 0) >= plan.grow - plan.main) & (
        lax.broadcasted_iota(jnp.int32, tail.shape, 1) >= plan.glane
    )
    tail_squares = jnp.where(is_gain, 1.0 / tp, 1.0) * tail * tail
    head = summed[: plan.main]
    squares = jnp.sum((head * head).reshape(-1, 8, LANES), axis=0)
    norm[0] = squares + jnp.sum(tail_squares.reshape(-1, 8, LANES), axis=0)

    def norm_copy(i):
        return remote(norm.at[0], norm.at[i], no_s.at[i], no_r.at[i], peer(i))

    @pl.loop(1, everyone)
    def _(i):
        norm_copy(i).start()

    @pl.loop(1, everyone)
    def _(i):
        norm_copy(i).wait()

    sum_squares = jnp.sum(jnp.sum(norm[...], axis=0), keepdims=True)
    rms = jnp.sqrt(jnp.broadcast_to(sum_squares, (1, LANES)) / count + 1e-06)
    factor = jnp.minimum(f32(1.0), 1.0 / rms)

    def update(gradient, p, first, second, decay):
        scaled = factor[:, : gradient.shape[1]] * gradient
        first_new = beta_first * first + (1.0 - beta_first) * scaled
        second_new = beta_second * second + (1.0 - beta_second) * scaled * scaled
        ratio = (first_new / (1.0 - beta_first**STEP)) / (
            jnp.sqrt(second_new / (1.0 - beta_second**STEP)) + 1e-08
        )
        return p - rate * (ratio + decay * p), first_new, second_new

    for j in range(plan.nq + plan.nl):
        query = j < plan.nq
        params = (pq, fq, sq) if query else (pl_, fl, sl)
        outs = (nq, mq, vq) if query else (nl, ml, vl)
        lane = LANES * (j if query else j - plan.nq)
        lo, size = (rp * j, rp) if query else (rp * plan.nq + wl * (j - plan.nq), wl)
        values = update(total[lo : lo + size], *(ref[:, lane : lane + LANES] for ref in params), 0.1)
        for ref, value in zip(outs, values):
            ref[:, lane : lane + LANES] = value
        ag[0, lo : lo + size] = values[0].astype(bf16)
    stage[...] = jnp.zeros(stage.shape, f32)
    for row, lane, source in plan.leftover():
        at = (pl.ds(source, 16), pl.ds(LANES * plan.nl, plan.left))
        values = update(total[row : row + 16, lane : lane + plan.left], pl_[at], fl[at], sl[at], 0.1)
        for ref, value in zip((nl, ml, vl), values):
            ref[at] = value
        stage[row - plan.main : row - plan.main + 16, lane : lane + plan.left] = values[0]
    gain_lanes = (slice(plan.grow, plan.grow + 1), slice(plan.glane, plan.glane + plan.gn))
    values = update(total[gain_lanes], pg[...], fg[...], sg[...], 0.0)
    for ref, value in zip((ng, mg, vg), values):
        ref[...] = value
    stage[plan.grow - plan.main : plan.grow - plan.main + 1, gain_lanes[1]] = values[0]
    ag[0, plan.main : plan.rows] = stage[...].astype(bf16)

    def ag_copy(half, step, d):
        k = plan.orders[half][step]
        source = d ^ (1 << k)
        index = plan.message(half, step, source if d >> k & 1 else d)
        lo, size = plan.halves[half]
        rows = pl.ds(lo, size)
        return remote(ag.at[d, rows], ag.at[source, rows], ag_s.at[index], ag_r.at[index], partner(k))

    def across(half, d):
        lo, size = plan.halves[half]
        rows = pl.ds(lo, size)
        index = half * m + d
        return remote(ag.at[d, rows], agc.at[d, rows], ac_s.at[index], ac_r.at[index], sibling)

    def arrived(half, step, d):
        for later in reversed(range(step)):
            ag_copy(half, later, d).start()
        across(half, d).start()

    def write(ref, d, block):
        for j in range(plan.nq):
            tq[block, :, LANES * j : LANES * (j + 1)] = ref[d, rp * j : rp * (j + 1)]
        for j in range(plan.nl):
            lo = rp * plan.nq + wl * j
            lat[:, LANES * j : LANES * (j + 1)] = ref[d, lo : lo + wl].astype(f32)
        last = ref[d, plan.main : plan.rows].astype(f32)
        for row, lane, source in plan.leftover():
            row -= plan.main
            lat[source : source + 16, LANES * plan.nl : LANES * plan.nl + plan.left] = last[
                row : row + 16, lane : lane + plan.left
            ]
        tile, start = plan.window(block)
        lanes = lax.broadcasted_iota(jnp.int32, lat.shape, 1)
        inside = (lanes >= start) & (lanes < start + plan.own_rows)
        tls[:, tile] = jnp.where(inside, pltpu.roll(lat[...], start, 1), tls[:, tile])
        tile, start = gain_window(block)
        row = plan.grow - plan.main
        gains = pltpu.roll(last[row : row + 8], (start - plan.glane + LANES) % LANES, 1)
        lanes = lax.broadcasted_iota(jnp.int32, gains.shape, 1)
        tgs[:, tile] = jnp.where((lanes >= start) & (lanes < start + plan.gn), gains, tgs[:, tile])

    for half in range(2):
        arrived(half, plan.bits, 0)
    write(ag, 0, mine(0))
    for step in reversed(range(plan.bits)):
        for half in range(2):
            k = plan.orders[half][step]
            for d in plan.slots_after(half, step):
                new = d | (1 << k)
                ag_copy(half, step, d).wait_recv()
                arrived(half, step, new)
    for d in range(1, m):
        write(ag, d, mine(d))
    for d in range(m):
        for half in range(2):
            across(half, d).wait_recv()
        write(agc, d, theirs(d))
    tl[...] = tls[...].astype(bf16)
    tg[...] = tgs[0:1].astype(bf16)

    for half in range(2):
        for step in range(plan.bits):
            k = plan.orders[half][step]
            for d in plan.slots_after(half, step):
                rs_copy(half, step, d | (1 << k)).wait_send()
                ag_copy(half, step, d).wait_send()
        for d in range(m):
            across(half, d).wait_send()


def hand_over(*refs):
    count = len(refs) // 2
    sems = refs[-1]
    copies = [pltpu.make_async_copy(refs[i], refs[count + i], sems.at[i]) for i in range(count)]
    for copy in copies:
        copy.start()
    for copy in copies:
        copy.wait()


def local(grad_query, grad_latent, grad_gains, *state):
    n, tp = lax.axis_size("fsdp"), lax.axis_size("tp")
    mb, _, depth, wq = grad_query.shape
    wl, gains = grad_latent.shape[3], grad_gains.shape[2]
    plan = Plan(n, tp, mb, depth // n, wq, wl, gains)
    count = depth * (wq + wl) * tp + gains
    extra = plan.rp - plan.own_rows

    def pad(x):
        return jnp.pad(x, [(0, 0)] * (x.ndim - 2) + [(0, extra), (0, 0)]) if extra else x

    query = pad(grad_query.reshape(mb, n, plan.own_rows, wq))
    latent = jnp.swapaxes(grad_latent[:, 0], 1, 2)
    kept = []
    for i in range(3):
        kept += [pad(state[3 * i]), state[3 * i + 1].T, state[3 * i + 2].reshape(1, plan.gn)]
    m, rp = plan.m, plan.rp
    vmem = pl.BlockSpec(memory_space=pltpu.VMEM)
    anywhere = pl.BlockSpec(memory_space=pl.ANY)
    out_shape = [
        jax.ShapeDtypeStruct(s, f32) for s in [(rp, wq), (wl, plan.own_rows), (1, plan.gn)] * 3
    ] + [jax.ShapeDtypeStruct(s, bf16) for s in [(n, rp, wq), (wl, depth), (1, gains)]]
    scratch = [
        pltpu.VMEM((m, mb, rp, wq), bf16),
        pltpu.VMEM((m, mb, wl, 2 * LANES), bf16),
        pltpu.VMEM((mb, 1, gains), bf16),
        pltpu.VMEM((8, gains), f32),
        pltpu.VMEM((m, plan.rows, LANES), f32),
        pltpu.VMEM((2 * (m - 1), max(s for _, s in plan.halves), LANES), f32),
        pltpu.VMEM((plan.rows, LANES), f32),
        pltpu.VMEM((plan.rows - plan.main, LANES), f32),
        pltpu.VMEM((n * tp, 8, LANES), f32),
        pltpu.VMEM((m, plan.rows, LANES), bf16),
        pltpu.VMEM((m, plan.rows, LANES), bf16),
        pltpu.VMEM((8, gains), f32),
        pltpu.VMEM((wl, depth), f32),
        pltpu.VMEM((wl, 2 * LANES), f32),
    ]
    planned = sum(math.prod(x.shape) * x.dtype.itemsize for x in scratch)
    outs = pl.pallas_call(
        functools.partial(kernel, plan, count),
        out_shape=out_shape,
        in_specs=[vmem] * 12,
        out_specs=[vmem] * 12,
        scratch_shapes=scratch
        + [
            pltpu.SemaphoreType.DMA((k,))
            for k in [m] * 4 + [1] * 2 + [2 * (m - 1)] * 2 + [n * tp] * 2 + [2 * (m - 1)] * 2 + [2 * m] * 2
        ],
        compiler_params=pltpu.CompilerParams(
            collective_id=0, has_side_effects=True, vmem_limit_bytes=max(planned + (14 << 20), 58 << 20)
        ),
    )(query, latent, grad_gains, *kept)
    outs = pl.pallas_call(
        hand_over,
        out_shape=out_shape,
        in_specs=[anywhere] * 12,
        out_specs=[anywhere] * 12,
        scratch_shapes=[pltpu.SemaphoreType.DMA((12,))],
        compiler_params=pltpu.CompilerParams(vmem_limit_bytes=58 << 20),
    )(*outs)
    result = []
    for i in range(3):
        result += [outs[3 * i][: plan.own_rows], outs[3 * i + 1].T, outs[3 * i + 2].reshape(plan.gn)]
    result += [outs[9][:, : plan.own_rows].reshape(depth, wq), outs[10].T, outs[11].reshape(gains)]
    return tuple(result)


def solution(mesh):
    shards = (P("fsdp", "tp"), P("fsdp", "tp"), P("fsdp"))
    in_specs = (P(None, "fsdp", None, "tp"), P(None, "fsdp", None, "tp"), P(None, "fsdp", None)) + shards * 3
    out_specs = shards * 3 + (P(None, "tp"), P(None, "tp"), P())
    return jax.shard_map(local, mesh=mesh, in_specs=in_specs, out_specs=out_specs, check_vma=False)
```
